32 devices in a mesh: seq: 8 (over z, y), mp: 4 (over x, core).
Axes of the slice: x: 2, y: 2, z: 4, core: 2. Of those that a mesh axis runs over, the one named last changes fastest.
Arguments:
- tokens: bfloat16 [16384, 2048], P('seq'), may hold values from -6 to 6
- w_proj: bfloat16 [2048, 4, 2048], P(None, None, 'mp')
- gain: float32 [2048], P('mp'), may hold values from 0.25 to 1.75
- level_codes: int32 [9, 16, 16384], P(None, 'mp', 'seq'), may hold values from 0 to 255
- w_codes: int32 [2048, 2048], P('mp'), may hold values from 40 to 199, as said below
- block_exponent: int32 [16, 16], P('mp'), may hold values from -7 to -5
Outputs:
- mixed: bfloat16 [16384, 2048], P(('seq', 'mp'))
The draws below stay inside these ranges and needn't reach their ends.
Inputs may be any that keep to these rules, and one draw needn't show every extreme that they name: `w_codes`: each code is 128 s + 8 e + m with s of 0 or 1, e from 5 to 8 and m from 0 to 7.
All inputs are finite; a program needn't handle non-finite values.
Results may differ from the reference program's by a relative error of at most 0.015.
Values may be sent and summed in bfloat16 or wider, within the bound.
A program may use at most 128 MiB of HBM per device.

```python
import math
import jax
import jax.numpy as jnp
from jax import lax

D = 2048
HEADS = 16
HEAD_DIM = 128
STRETCH = 64
BLOCK = 128
HD = 2048
TOKENS = 16384
LEVELS = 9
N_MP = 4


def draw_w_proj(key, part):
    first, second = jax.random.split(jax.random.fold_in(key, 11), 2)
    width = HEADS * HEAD_DIM
    column_scale = jnp.exp(jax.random.uniform(first, (1, 4, width), jnp.float32, math.log(0.3), math.log(3.0)))
    base = jax.random.normal(second, (D, 4, width), jnp.float32)
    return (base * column_scale / math.sqrt(D)).astype(jnp.bfloat16)


def draw_w_codes(key, part):
    first, second, third = jax.random.split(jax.random.fold_in(key, 23), 3)
    width = HEADS * HEAD_DIM
    negative = jax.random.randint(first, (width, D), 0, 2, jnp.int32)
    exponent = jax.random.randint(second, (width, D), 5, 9, jnp.int32)
    mantissa = jax.random.randint(third, (width, D), 0, 8, jnp.int32)
    return 128 * negative + 8 * exponent + mantissa


def plant(values, rng, least, high):
    longest = values.shape.index(max(values.shape))
    spots = []
    for shift in (0, 1):
        where = [jax.random.randint(jax.random.fold_in(rng, axis), (), 0, length) for axis, length in enumerate(values.shape)]
        where[longest] = (where[longest] + shift) % values.shape[longest]
        spots.append(tuple(where))
    return values.at[spots[0]].set(least).at[spots[1]].set(high)


def block_scale(key, dims, cuts, smallest, largest):
    loudness = 1.0
    for axis_at, blocks in cuts:
        draws = jax.random.uniform(jax.random.fold_in(jax.random.fold_in(key, 6), axis_at), (blocks,), jnp.float32, smallest / len(cuts), largest / len(cuts))
        loudness = loudness * jnp.repeat(jnp.exp(draws), dims[axis_at] // blocks).reshape((-1,) + (1,) * (len(dims) - 1 - axis_at))
    return loudness


def gaussian(rng, extent, spread, bound, cuts=(), dtype=jnp.bfloat16):
    level = block_scale(rng, extent, cuts, -0.22, 0.18) if cuts else 1.0
    entries = jax.random.normal(rng, extent, jnp.float32) * spread * level
    return jnp.minimum(jnp.maximum(entries, -bound), bound).astype(dtype)


def setup_inputs(seed: int = 0) -> dict:
    key_list = jax.random.split(jax.random.key(seed), 7)
    tokens = gaussian(key_list[0], (TOKENS, D), 1.0, 6.0, ((0, 8),))
    w_proj = draw_w_proj(jax.random.fold_in(key_list[6], 71), 0)
    gain = jnp.clip(1.0 + 0.15 * jax.random.normal(key_list[2], (HD,), jnp.float32), 0.25, 1.75)
    level_codes = plant(jax.random.randint(key_list[3], (LEVELS, HEADS, TOKENS), 0, 256), jax.random.fold_in(key_list[3], 1), 0, 255).astype(jnp.int32)
    w_codes = draw_w_codes(jax.random.fold_in(key_list[6], 71), 0)
    block_exponent = plant(jax.random.randint(key_list[5], (HD // BLOCK, D // BLOCK), -7, -4), jax.random.fold_in(key_list[5], 1), -7, (-4) - 1).astype(jnp.int32)
    return dict(tokens=tokens, w_proj=w_proj, gain=gain, level_codes=level_codes, w_codes=w_codes, block_exponent=block_exponent)


def power_of_two(field, bits):
    result = jnp.ones(field.shape, jnp.float32)
    for bit in range(bits):
        result = result * jnp.where(field // 2 ** bit % 2 == 1, jnp.float32(2.0 ** 2 ** bit), jnp.float32(1.0))
    return result

def decode_weight(codes, exponents, block):
    negative = codes // 128
    exponent = codes // 8 % 16
    mantissa = codes % 8
    magnitude = (8 + mantissa).astype(jnp.float32) * (1 - 2 * negative).astype(jnp.float32)
    magnitude = magnitude * power_of_two(exponent, 4) * jnp.float32(2.0 ** (-10))
    scales = power_of_two(exponents + 16, 5) * jnp.float32(2.0 ** (-16))
    rows, columns = codes.shape
    shaped = magnitude.reshape(rows // block, block, columns // block, block) * scales[:, None, :, None]
    return shaped.reshape(rows, columns).astype(jnp.bfloat16)

def head_mix(inputs):
    query, keys, values, level_weight = inputs
    stretches = TOKENS // STRETCH
    query_blocks = query.reshape(stretches, STRETCH, HEAD_DIM)
    key_blocks = keys.reshape(stretches, STRETCH, HEAD_DIM).astype(jnp.float32)
    value_blocks = values.reshape(stretches, STRETCH, HEAD_DIM).astype(jnp.float32)
    scores = jnp.einsum('ntd,nsd->nts', query_blocks.astype(jnp.float32), key_blocks)
    causal = jnp.tril(jnp.ones((STRETCH, STRETCH), bool))
    weights = (jnp.where(causal[None], scores, 0.0) * (1.0 / math.sqrt(HEAD_DIM * STRETCH))).astype(jnp.bfloat16)
    local = jnp.einsum('nts,nsd->ntd', weights.astype(jnp.float32), value_blocks)
    total = level_weight[0].reshape(stretches, STRETCH)[:, :, None] * local
    blocks = jnp.einsum('ntd,nte->nde', key_blocks, value_blocks)
    for level in range(LEVELS - 1):
        count = stretches >> level + 1
        span = STRETCH << level
        pairs = blocks.reshape(count, 2, HEAD_DIM, HEAD_DIM)
        sibling = pairs[:, 0].astype(jnp.bfloat16)
        second = query_blocks.reshape(count, 2, span, HEAD_DIM)[:, 1]
        term = jnp.einsum('ptd,pde->pte', second.astype(jnp.float32), sibling.astype(jnp.float32))
        term = term * (1.0 / math.sqrt(HEAD_DIM * span))
        weight_second = level_weight[level + 1].reshape(count, 2, span)[:, 1]
        placed = jnp.stack([jnp.zeros_like(term), weight_second[:, :, None] * term], 1)
        total = total + placed.reshape(stretches, STRETCH, HEAD_DIM)
        blocks = pairs[:, 0] + pairs[:, 1]
    return total.reshape(TOKENS, HEAD_DIM)

def reference(tokens, w_proj, gain, level_codes, w_codes, block_exponent):
    width = HEADS * HEAD_DIM
    projected = jnp.dot(tokens, w_proj.reshape(D, 4 * width), preferred_element_type=jnp.float32)
    projected = projected.reshape(TOKENS, 4, HEADS, HEAD_DIM)
    query = projected[:, 0].astype(jnp.bfloat16).transpose(1, 0, 2)
    keys = projected[:, 1].astype(jnp.bfloat16).transpose(1, 0, 2)
    values = projected[:, 2].astype(jnp.bfloat16).transpose(1, 0, 2)
    gate = jax.nn.silu(projected[:, 3].reshape(TOKENS, width))
    level_weight = (level_codes.astype(jnp.float32) / 128.0).transpose(1, 0, 2)
    memory = lax.map(head_mix, (query, keys, values, level_weight)).transpose(1, 0, 2)
    normed = memory * lax.rsqrt(lax.optimization_barrier(jnp.mean(memory * memory, axis=-1, keepdims=True)) + 1e-06)
    attended = (normed.reshape(TOKENS, width) * gain * gate).astype(jnp.bfloat16)
    weight = decode_weight(w_codes, block_exponent, BLOCK)
    group = width // N_MP
    mixed = jnp.zeros((TOKENS, D), jnp.float32)
    for member in range(N_MP):
        partial_value = jnp.dot(attended[:, member * group:(member + 1) * group], weight[member * group:(member + 1) * group], preferred_element_type=jnp.float32).astype(jnp.bfloat16)
        partial_value = lax.optimization_barrier(partial_value)
        mixed = mixed + partial_value.astype(jnp.float32)
    return mixed.astype(jnp.bfloat16)
```

```python
import functools
import math

import jax
import jax.numpy as jnp
from jax import lax
from jax.experimental import pallas as pl
from jax.experimental.pallas import tpu as pltpu
from jax.sharding import PartitionSpec as P

HEAD_DIM = 128
STRETCH = 64
BLOCK = 128
CORES = 2
QB = 256
MESH = pl.DeviceIdType.MESH
F32 = jnp.float32
BF16 = jnp.bfloat16


def power_of_two(field, bits):
    result = jnp.ones(field.shape, jnp.float32)
    for bit in range(bits):
        result = result * jnp.where(
            field // 2**bit % 2 == 1, jnp.float32(2.0**2**bit), jnp.float32(1.0)
        )
    return result


def dot(a, b):
    return jnp.dot(a, b, preferred_element_type=F32)


def dot_nt(a, b):
    return lax.dot_general(a, b, (((1,), (1,)), ((), ())), preferred_element_type=F32)


def dot_tn(a, b):
    return lax.dot_general(a, b, (((0,), (0,)), ((), ())), preferred_element_type=F32)


def kernel(
    cfg,
    tok_hbm, w_hbm, codes_hbm, gain_ref, lw_ref, scale_ref,
    out_ref,
    tok, wj, wstage, cstage, wfull, kv, q, gate, att, attr, local, tot, snd, rcv, masks, acc,
    tok_sem, w_sem, c_sem, ws_sem, wr_sem, as_sem, ar_sem, ss_sem, sr_sem,
):
    groups, seq_bits, block_bits, in_bits = cfg
    rows_all, width = q.shape
    depth = tok.shape[1]
    heads = width // HEAD_DIM
    rows = rows_all // groups
    chips = groups // CORES
    seq = lax.axis_index("seq")
    mp = lax.axis_index("mp")
    x = mp // CORES
    c = mp % CORES

    def peer(ix, kc):
        return ((x + ix) % chips) * CORES + (c + kc) % CORES

    def source(ix, kc):
        return ((x - ix + chips) % chips) * CORES + (c - kc + CORES) % CORES

    def seq_peer(j):
        bit = (seq // 2**j) % 2
        return seq + 2**j - bit * 2 ** (j + 1)

    crows = cstage.shape[1]
    wrows = wstage.shape[1]
    n_c = width // crows
    n_w = depth // wrows

    def c_copy(i):
        slot = i % 2
        return pltpu.make_async_copy(
            codes_hbm.at[pl.ds(i * crows, crows)], cstage.at[slot], c_sem.at[slot]
        )

    def w_copy(i):
        slot = i % 2
        return pltpu.make_async_copy(
            w_hbm.at[pl.ds(i * wrows, wrows)], wstage.at[slot], w_sem.at[slot]
        )

    for i in range(2):
        c_copy(i).start()
    for i in range(2):
        w_copy(i).start()
    tok_copy = pltpu.make_async_copy(tok_hbm, tok, tok_sem)
    tok_copy.start()

    barrier = pltpu.get_barrier_semaphore()
    for r in range(1, groups):
        pl.semaphore_signal(
            barrier, inc=1, device_id=(seq, peer(r // CORES, r % CORES)), device_id_type=MESH
        )
    for j in range(seq_bits):
        pl.semaphore_signal(barrier, inc=1, device_id=(seq_peer(j), mp), device_id_type=MESH)

    @pl.loop(0, n_c)
    def _(i):
        c_copy(i).wait()
        codes = cstage[i % 2]
        whole = ((codes & 7) | 8) << ((codes >> 3) & 15)
        value = whole.astype(F32)
        value = jnp.where(codes >= 128, -value, value) * scale_ref[pl.ds(i, 1), :]
        wfull[mp, pl.ds(pl.multiple_of(i * crows, crows), crows), :] = value.astype(BF16)

        @pl.when(i + 2 < n_c)
        def _():
            c_copy(i + 2).start()

    t = lax.broadcasted_iota(jnp.int32, (QB, QB), 0)
    s = lax.broadcasted_iota(jnp.int32, (QB, QB), 1)
    tc = t // STRETCH
    sc = s // STRETCH
    masks[0] = jnp.where((tc == sc) & (s <= t), 1.0, 0.0).astype(F32)
    for j in range(in_bits):
        hit = ((tc // 2**j) % 2 == 1) & (sc // 2**j == tc // 2**j - 1)
        masks[j + 1] = jnp.where(hit, 1.0, 0.0).astype(F32)

    pl.semaphore_wait(barrier, groups - 1 + seq_bits)

    def w_send(k, shard, target):
        return pltpu.make_async_remote_copy(
            src_ref=wfull.at[shard], dst_ref=wfull.at[shard],
            send_sem=ws_sem.at[k], recv_sem=wr_sem.at[k],
            device_id=(seq, target), device_id_type=MESH,
        )

    for ix in range(1, chips):
        w_send(ix, mp, peer(ix, 0)).start()
    w_send(0, mp, peer(0, 1)).start()

    @pl.loop(0, n_w)
    def _(i):
        w_copy(i).wait()
        wj[:, pl.ds(pl.multiple_of(i * wrows, wrows), wrows), :] = jnp.swapaxes(wstage[i % 2], 0, 1)

        @pl.when(i + 2 < n_w)
        def _():
            w_copy(i + 2).start()

    tok_copy.wait()
    tb = min(512, rows_all)
    n_t = rows_all // tb

    @pl.loop(0, 2 * n_t)
    def _(i):
        part = i // n_t
        at = pl.ds(pl.multiple_of((i % n_t) * tb, tb), tb)
        kv[part, at, :] = dot(tok[at, :], wj[1 + part]).astype(BF16)

    n_b = rows_all // QB

    @pl.loop(0, heads)
    def _(h):
        cols = pl.ds(pl.multiple_of(h * HEAD_DIM, HEAD_DIM), HEAD_DIM)
        level = []
        for b in range(n_b):
            at = pl.ds(b * QB, QB)
            level.append(dot_tn(kv[0, at, cols], kv[1, at, cols]))
        base = 0
        while len(level) > 1:
            for b, state in enumerate(level):
                local[base + b, h] = state.astype(BF16)
            base += len(level)
            level = [level[2 * b] + level[2 * b + 1] for b in range(len(level) // 2)]
        tot[h] = level[0]
        snd[0, h] = level[0].astype(BF16)

    def s_send(j):
        return pltpu.make_async_remote_copy(
            src_ref=snd.at[j], dst_ref=rcv.at[j],
            send_sem=ss_sem.at[j], recv_sem=sr_sem.at[j],
            device_id=(seq_peer(j), mp), device_id_type=MESH,
        )

    s_send(0).start()

    def exchange(j):
        s_send(j).wait_recv()
        if j + 1 < seq_bits:
            total = tot[...] + rcv[j].astype(F32)
            tot[...] = total
            snd[j + 1] = total.astype(BF16)
            s_send(j + 1).start()

    @pl.loop(0, n_t)
    def _(i):
        at = pl.ds(pl.multiple_of(i * tb, tb), tb)
        q[at, :] = dot(tok[at, :], wj[0]).astype(BF16)
        g = dot(tok[at, :], wj[3])
        gate[at, :] = g / (1.0 + jnp.exp(-g)) * gain_ref[...]
        for j in range(min(seq_bits, n_t)):
            @pl.when(i == j)
            def _(j=j):
                exchange(j)

    for j in range(n_t, seq_bits):
        exchange(j)

    def a_send(r, target):
        at = pl.ds(pl.multiple_of(target * rows, rows), rows)
        return pltpu.make_async_remote_copy(
            src_ref=att.at[at], dst_ref=attr.at[mp],
            send_sem=as_sem.at[r], recv_sem=ar_sem.at[r],
            device_id=(seq, target), device_id_type=MESH,
        )

    n_in = 1 + in_bits

    @pl.loop(0, groups)
    def _(step):
        r = groups - 1 - step
        owner = peer(r // CORES, r % CORES)

        @pl.loop(0, rows // QB)
        def _(part):
            b = owner * (rows // QB) + part
            at = pl.ds(pl.multiple_of(b * QB, QB), QB)
            for h in range(heads):
                cols = slice(h * HEAD_DIM, (h + 1) * HEAD_DIM)
                qh = q[at, cols]

                def weight(level):
                    k = level * heads + h
                    return lw_ref[at, k : k + 1]

                scores = dot_nt(qh, kv[0, at, cols])
                mix = weight(0) * masks[0]
                for j in range(in_bits):
                    mix = mix + weight(1 + j) * masks[1 + j]
                left = [(scores * mix).astype(BF16)]
                right = [kv[1, at, cols]]
                qf = qh.astype(F32)
                base = 0
                for j in range(block_bits):
                    node = b // 2**j
                    bit = node % 2
                    left.append((qf * (weight(n_in + j) * bit.astype(F32))).astype(BF16))
                    right.append(local[base + node - bit, h])
                    base += n_b >> j
                for j in range(seq_bits):
                    bit = (seq // 2**j) % 2
                    left.append((qf * (weight(n_in + block_bits + j) * bit.astype(F32))).astype(BF16))
                    right.append(rcv[j, h])
                memory = dot(jnp.concatenate(left, 1), jnp.concatenate(right, 0))
                mean = jnp.mean(memory * memory, axis=-1, keepdims=True)
                att[at, cols] = (memory * lax.rsqrt(mean + 1e-06) * gate[at, cols]).astype(BF16)

        @pl.when(r > 0)
        def _():
            a_send(r, owner).start()

    for ix in range(1, chips):
        shard = source(ix, 0)
        w_send(ix, shard, mp_other(x, c)).wait_recv()
        w_send(chips - 1 + ix, shard, peer(0, 1)).start()

    nb = min(512, depth)

    def product(left, g, first, last):
        @pl.loop(0, depth // nb)
        def _(i):
            cols = pl.ds(pl.multiple_of(i * nb, nb), nb)
            value = dot(left, wfull[g, :, cols])
            if not first:
                value = value + acc[:, cols]
            if last:
                out_ref[:, cols] = value.astype(BF16)
            else:
                acc[:, cols] = value

    own = pl.ds(pl.multiple_of(mp * rows, rows), rows)
    product(att[own, :], mp, True, groups == 1)
    for r in range(1, groups):
        ix, kc = r // CORES, r % CORES
        src = source(ix, kc)
        at = pl.ds(pl.multiple_of(src * rows, rows), rows)
        pltpu.make_async_remote_copy(
            src_ref=att.at[own], dst_ref=attr.at[src],
            send_sem=as_sem.at[r], recv_sem=ar_sem.at[r],
            device_id=(seq, src), device_id_type=MESH,
        ).wait_recv()
        if kc:
            k = 0 if ix == 0 else chips - 1 + ix
            w_send(k, src, src).wait_recv()
        product(attr[src], src, False, r == groups - 1)

    w_send(0, mp, peer(0, 1)).wait_send()
    for ix in range(1, chips):
        w_send(ix, mp, peer(ix, 0)).wait_send()
        w_send(chips - 1 + ix, source(ix, 0), peer(0, 1)).wait_send()
    for j in range(seq_bits):
        s_send(j).wait_send()
    for r in range(1, groups):
        a_send(r, peer(r // CORES, r % CORES)).wait_send()


def mp_other(x, c):
    return x * CORES + (c + 1) % CORES


def body(tokens, w_proj, gain, level_codes, w_codes, block_exponent):
    rows_all, depth = tokens.shape
    width = w_proj.shape[2]
    heads = width // HEAD_DIM
    groups = lax.axis_size("mp")
    seq_size = lax.axis_size("seq")
    seq_bits = seq_size.bit_length() - 1
    stretch_bits = (rows_all // STRETCH).bit_length() - 1
    in_bits = (QB // STRETCH).bit_length() - 1
    block_bits = stretch_bits - in_bits
    levels = level_codes.shape[0]
    rows = rows_all // groups
    chips = groups // CORES
    spans = [STRETCH] + [STRETCH << j for j in range(levels - 1)]
    factors = jnp.array([1.0 / 128.0 / math.sqrt(HEAD_DIM * span) for span in spans], F32)
    level_weight = (level_codes.astype(F32) * factors[:, None, None]).reshape(
        levels * heads, rows_all
    ).T
    scales = power_of_two(block_exponent + 16, 5) * jnp.float32(2.0 ** (-26))
    scales = jnp.repeat(scales, BLOCK, axis=1)
    n_b = rows_all // QB
    vmem = pl.BlockSpec(memory_space=pltpu.VMEM)
    hbm = pl.BlockSpec(memory_space=pl.ANY)
    dma = pltpu.SemaphoreType.DMA
    return pl.pallas_call(
        functools.partial(kernel, (groups, seq_bits, block_bits, in_bits)),
        out_shape=jax.ShapeDtypeStruct((rows, depth), BF16),
        in_specs=[hbm, hbm, hbm, vmem, vmem, vmem],
        out_specs=vmem,
        scratch_shapes=[
            pltpu.VMEM((rows_all, depth), BF16),
            pltpu.VMEM((4, depth, width), BF16),
            pltpu.VMEM((2, 256, 4, width), BF16),
            pltpu.VMEM((2, BLOCK, depth), jnp.int32),
            pltpu.VMEM((groups, width, depth), BF16),
            pltpu.VMEM((2, rows_all, width), BF16),
            pltpu.VMEM((rows_all, width), BF16),
            pltpu.VMEM((rows_all, width), F32),
            pltpu.VMEM((rows_all, width), BF16),
            pltpu.VMEM((groups, rows, width), BF16),
            pltpu.VMEM((2 * n_b, heads, HEAD_DIM, HEAD_DIM), BF16),
            pltpu.VMEM((heads, HEAD_DIM, HEAD_DIM), F32),
            pltpu.VMEM((seq_bits, heads, HEAD_DIM, HEAD_DIM), BF16),
            pltpu.VMEM((seq_bits, heads, HEAD_DIM, HEAD_DIM), BF16),
            pltpu.VMEM((1 + in_bits, QB, QB), F32),
            pltpu.VMEM((rows, depth), F32),
            dma, dma((2,)), dma((2,)),
            dma((2 * chips - 1,)), dma((2 * chips - 1,)),
            dma((groups,)), dma((groups,)),
            dma((seq_bits,)), dma((seq_bits,)),
        ],
        compiler_params=pltpu.CompilerParams(
            collective_id=0, has_side_effects=True, vmem_limit_bytes=67043328
        ),
        name="layer",
    )(tokens, w_proj, w_codes, gain.reshape(1, width), level_weight, scales)


def solution(mesh):
    placed = (
        P("seq", None),
        P(None, None, "mp"),
        P("mp"),
        P(None, "mp", "seq"),
        P("mp", None),
        P("mp", None),
    )
    return jax.shard_map(
        body, mesh=mesh, in_specs=placed, out_specs=P(("seq", "mp"), None), check_vma=False
    )
```

```python
import functools
import math

import jax
import jax.numpy as jnp
from jax import lax
from jax.experimental import pallas as pl
from jax.experimental.pallas import tpu as pltpu
from jax.sharding import PartitionSpec as P

HEAD_DIM = 128
STRETCH = 64
BLOCK = 128
CORES = 2
QB = 256
MESH = pl.DeviceIdType.MESH
F32 = jnp.float32
BF16 = jnp.bfloat16


def power_of_two(field, bits):
    result = jnp.ones(field.shape, jnp.float32)
    for bit in range(bits):
        result = result * jnp.where(
            field // 2**bit % 2 == 1, jnp.float32(2.0**2**bit), jnp.float32(1.0)
        )
    return result


def dot(a, b):
    return jnp.dot(a, b, preferred_element_type=F32)


def dot_nt(a, b):
    return lax.dot_general(a, b, (((1,), (1,)), ((), ())), preferred_element_type=F32)


def dot_tn(a, b):
    return lax.dot_general(a, b, (((0,), (0,)), ((), ())), preferred_element_type=F32)


def kernel(
    cfg,
    tok_hbm, w_hbm, codes_hbm, gain_ref, lw_ref, scale_ref,
    out_ref,
    tok, wj, wstage, cstage, wfull, kv, q, gate, att, attr, local, tot, snd, rcv, masks, acc,
    tok_sem, w_sem, c_sem, ws_sem, wr_sem, as_sem, ar_sem, ss_sem, sr_sem,
):
    groups, seq_bits, block_bits, in_bits = cfg
    rows_all, width = q.shape
    depth = tok.shape[1]
    heads = width // HEAD_DIM
    rows = rows_all // groups
    chips = groups // CORES
    seq = lax.axis_index("seq")
    mp = lax.axis_index("mp")
    x = mp // CORES
    c = mp % CORES

    def peer(ix, kc):
        return ((x + ix) % chips) * CORES + (c + kc) % CORES

    def source(ix, kc):
        return ((x - ix + chips) % chips) * CORES + (c - kc + CORES) % CORES

    def seq_peer(j):
        bit = (seq // 2**j) % 2
        return seq + 2**j - bit * 2 ** (j + 1)

    crows = cstage.shape[1]
    wrows = wstage.shape[1]
    n_c = width // crows
    n_w = depth // wrows

    def c_copy(i):
        slot = i % 2
        return pltpu.make_async_copy(
            codes_hbm.at[pl.ds(i * crows, crows)], cstage.at[slot], c_sem.at[slot]
        )

    def w_copy(i):
        slot = i % 2
        return pltpu.make_async_copy(
            w_hbm.at[pl.ds(i * wrows, wrows)], wstage.at[slot], w_sem.at[slot]
        )

    for i in range(2):
        c_copy(i).start()
    for i in range(2):
        w_copy(i).start()
    tok_copy = pltpu.make_async_copy(tok_hbm, tok, tok_sem)
    tok_copy.start()

    barrier = pltpu.get_barrier_semaphore()
    for r in range(1, groups):
        pl.semaphore_signal(
            barrier, inc=1, device_id=(seq, peer(r // CORES, r % CORES)), device_id_type=MESH
        )
    for j in range(seq_bits):
        pl.semaphore_signal(barrier, inc=1, device_id=(seq_peer(j), mp), device_id_type=MESH)

    @pl.loop(0, n_c)
    def _(i):
        c_copy(i).wait()
        codes = cstage[i % 2]
        whole = ((codes & 7) | 8) << ((codes >> 3) & 15)
        value = whole.astype(F32)
        value = jnp.where(codes >= 128, -value, value) * scale_ref[pl.ds(i, 1), :]
        wfull[mp, pl.ds(pl.multiple_of(i * crows, crows), crows), :] = value.astype(BF16)

        @pl.when(i + 2 < n_c)
        def _():
            c_copy(i + 2).start()

    t = lax.broadcasted_iota(jnp.int32, (QB, QB), 0)
    s = lax.broadcasted_iota(jnp.int32, (QB, QB), 1)
    tc = t // STRETCH
    sc = s // STRETCH
    masks[0] = jnp.where((tc == sc) & (s <= t), 1.0, 0.0).astype(F32)
    for j in range(in_bits):
        hit = ((tc // 2**j) % 2 == 1) & (sc // 2**j == tc // 2**j - 1)
        masks[j + 1] = jnp.where(hit, 1.0, 0.0).astype(F32)

    pl.semaphore_wait(barrier, groups - 1 + seq_bits)

    n_x = chips - 1
    parity = seq % 2
    half = width // 2
    piece = half // 2

    def w_send(k, shard, start, size, seq_to, mp_to):
        at = pl.ds(pl.multiple_of(start, piece), size)
        return pltpu.make_async_remote_copy(
            src_ref=wfull.at[shard, at], dst_ref=wfull.at[shard, at],
            send_sem=ws_sem.at[k], recv_sem=wr_sem.at[k],
            device_id=(seq_to, mp_to), device_id_type=MESH,
        )

    def x_part(ix, ch, shard):
        return w_send(2 * (ix - 1) + ch, shard, parity * half + ch * piece, piece, seq, peer(ix, 0))

    def y_part(ix, ch, which):
        k = 2 * n_x + 2 * (ix - 1) + ch
        return w_send(k, source(ix, 0), which * half + ch * piece, piece, seq_peer(0), mp)

    def cx_part(ix, ch, kc):
        k = 4 * n_x + 2 * (ix - 1) + ch
        return w_send(k, source(ix, kc), parity * half + ch * piece, piece, seq, peer(0, 1))

    def cy_part(ix, kc):
        return w_send(6 * n_x + ix - 1, source(ix, kc), (1 - parity) * half, half, seq, peer(0, 1))

    def c_part(shard):
        return w_send(7 * n_x, shard, 0, width, seq, peer(0, 1))

    def relay(ch):
        for ix in range(1, chips):
            x_part(ix, ch, source(ix, 0)).wait_recv()
            y_part(ix, ch, parity).start()
            cx_part(ix, ch, 0).start()

    for ch in range(2):
        for ix in range(1, chips):
            x_part(ix, ch, mp).start()
    c_part(mp).start()

    @pl.loop(0, n_w)
    def _(i):
        w_copy(i).wait()
        wj[:, pl.ds(pl.multiple_of(i * wrows, wrows), wrows), :] = jnp.swapaxes(wstage[i % 2], 0, 1)

        @pl.when(i + 2 < n_w)
        def _():
            w_copy(i + 2).start()

    tok_copy.wait()
    tb = min(512, rows_all)
    n_t = rows_all // tb

    @pl.loop(0, 2 * n_t)
    def _(i):
        part = i // n_t
        at = pl.ds(pl.multiple_of((i % n_t) * tb, tb), tb)
        kv[part, at, :] = dot(tok[at, :], wj[1 + part]).astype(BF16)

    n_b = rows_all // QB

    @pl.loop(0, heads)
    def _(h):
        cols = pl.ds(pl.multiple_of(h * HEAD_DIM, HEAD_DIM), HEAD_DIM)
        level = []
        for b in range(n_b):
            at = pl.ds(b * QB, QB)
            level.append(dot_tn(kv[0, at, cols], kv[1, at, cols]))
        base = 0
        while len(level) > 1:
            for b, state in enumerate(level):
                local[base + b, h] = state.astype(BF16)
            base += len(level)
            level = [level[2 * b] + level[2 * b + 1] for b in range(len(level) // 2)]
        tot[h] = level[0]
        snd[0, h] = level[0].astype(BF16)

    def s_send(j):
        return pltpu.make_async_remote_copy(
            src_ref=snd.at[j], dst_ref=rcv.at[j],
            send_sem=ss_sem.at[j], recv_sem=sr_sem.at[j],
            device_id=(seq_peer(j), mp), device_id_type=MESH,
        )

    s_send(0).start()
    relay(0)

    def exchange(j):
        s_send(j).wait_recv()
        if j + 1 < seq_bits:
            total = tot[...] + rcv[j].astype(F32)
            tot[...] = total
            snd[j + 1] = total.astype(BF16)
            s_send(j + 1).start()

    @pl.loop(0, n_t)
    def _(i):
        at = pl.ds(pl.multiple_of(i * tb, tb), tb)
        q[at, :] = dot(tok[at, :], wj[0]).astype(BF16)
        g = dot(tok[at, :], wj[3])
        gate[at, :] = g / (1.0 + jnp.exp(-g)) * gain_ref[...]
        for j in range(min(seq_bits, n_t)):
            @pl.when(i == j)
            def _(j=j):
                exchange(j)

    for j in range(n_t, seq_bits):
        exchange(j)

    relay(1)

    def a_send(r, target):
        at = pl.ds(pl.multiple_of(target * rows, rows), rows)
        return pltpu.make_async_remote_copy(
            src_ref=att.at[at], dst_ref=attr.at[mp],
            send_sem=as_sem.at[r], recv_sem=ar_sem.at[r],
            device_id=(seq, target), device_id_type=MESH,
        )

    n_in = 1 + in_bits

    @pl.loop(0, groups)
    def _(step):
        r = groups - 1 - step
        owner = peer(r // CORES, r % CORES)

        @pl.loop(0, rows // QB)
        def _(part):
            b = owner * (rows // QB) + part
            at = pl.ds(pl.multiple_of(b * QB, QB), QB)
            for h in range(heads):
                cols = slice(h * HEAD_DIM, (h + 1) * HEAD_DIM)
                qh = q[at, cols]

                def weight(level):
                    k = level * heads + h
                    return lw_ref[at, k : k + 1]

                scores = dot_nt(qh, kv[0, at, cols])
                mix = weight(0) * masks[0]
                for j in range(in_bits):
                    mix = mix + weight(1 + j) * masks[1 + j]
                left = [(scores * mix).astype(BF16)]
                right = [kv[1, at, cols]]
                qf = qh.astype(F32)
                base = 0
                for j in range(block_bits):
                    node = b // 2**j
                    bit = node % 2
                    left.append((qf * (weight(n_in + j) * bit.astype(F32))).astype(BF16))
                    right.append(local[base + node - bit, h])
                    base += n_b >> j
                for j in range(seq_bits):
                    bit = (seq // 2**j) % 2
                    left.append((qf * (weight(n_in + block_bits + j) * bit.astype(F32))).astype(BF16))
                    right.append(rcv[j, h])
                memory = dot(jnp.concatenate(left, 1), jnp.concatenate(right, 0))
                mean = jnp.mean(memory * memory, axis=-1, keepdims=True)
                att[at, cols] = (memory * lax.rsqrt(mean + 1e-06) * gate[at, cols]).astype(BF16)

        @pl.when(r > 0)
        def _():
            a_send(r, owner).start()

    for ix in range(1, chips):
        for ch in range(2):
            y_part(ix, ch, 1 - parity).wait_recv()
        cy_part(ix, 0).start()

    nb = min(512, depth)

    def product(left, g, first, last):
        @pl.loop(0, depth // nb)
        def _(i):
            cols = pl.ds(pl.multiple_of(i * nb, nb), nb)
            value = dot(left, wfull[g, :, cols])
            if not first:
                value = value + acc[:, cols]
            if last:
                out_ref[:, cols] = value.astype(BF16)
            else:
                acc[:, cols] = value

    own = pl.ds(pl.multiple_of(mp * rows, rows), rows)
    product(att[own, :], mp, True, groups == 1)
    for r in range(1, groups):
        ix, kc = r // CORES, r % CORES
        src = source(ix, kc)
        at = pl.ds(pl.multiple_of(src * rows, rows), rows)
        pltpu.make_async_remote_copy(
            src_ref=att.at[own], dst_ref=attr.at[src],
            send_sem=as_sem.at[r], recv_sem=ar_sem.at[r],
            device_id=(seq, src), device_id_type=MESH,
        ).wait_recv()
        if kc and ix:
            for ch in range(2):
                cx_part(ix, ch, 1).wait_recv()
            cy_part(ix, 1).wait_recv()
        elif kc:
            c_part(src).wait_recv()
        product(attr[src], src, False, r == groups - 1)

    c_part(mp).wait_send()
    for ix in range(1, chips):
        for ch in range(2):
            x_part(ix, ch, mp).wait_send()
            y_part(ix, ch, parity).wait_send()
            cx_part(ix, ch, 0).wait_send()
        cy_part(ix, 0).wait_send()
    for j in range(seq_bits):
        s_send(j).wait_send()
    for r in range(1, groups):
        a_send(r, peer(r // CORES, r % CORES)).wait_send()


def body(tokens, w_proj, gain, level_codes, w_codes, block_exponent):
    rows_all, depth = tokens.shape
    width = w_proj.shape[2]
    heads = width // HEAD_DIM
    groups = lax.axis_size("mp")
    seq_size = lax.axis_size("seq")
    seq_bits = seq_size.bit_length() - 1
    stretch_bits = (rows_all // STRETCH).bit_length() - 1
    in_bits = (QB // STRETCH).bit_length() - 1
    block_bits = stretch_bits - in_bits
    levels = level_codes.shape[0]
    rows = rows_all // groups
    chips = groups // CORES
    spans = [STRETCH] + [STRETCH << j for j in range(levels - 1)]
    factors = jnp.array([1.0 / 128.0 / math.sqrt(HEAD_DIM * span) for span in spans], F32)
    level_weight = (level_codes.astype(F32) * factors[:, None, None]).reshape(
        levels * heads, rows_all
    ).T
    scales = power_of_two(block_exponent + 16, 5) * jnp.float32(2.0 ** (-26))
    scales = jnp.repeat(scales, BLOCK, axis=1)
    n_b = rows_all // QB
    vmem = pl.BlockSpec(memory_space=pltpu.VMEM)
    hbm = pl.BlockSpec(memory_space=pl.ANY)
    dma = pltpu.SemaphoreType.DMA
    return pl.pallas_call(
        functools.partial(kernel, (groups, seq_bits, block_bits, in_bits)),
        out_shape=jax.ShapeDtypeStruct((rows, depth), BF16),
        in_specs=[hbm, hbm, hbm, vmem, vmem, vmem],
        out_specs=vmem,
        scratch_shapes=[
            pltpu.VMEM((rows_all, depth), BF16),
            pltpu.VMEM((4, depth, width), BF16),
            pltpu.VMEM((2, 256, 4, width), BF16),
            pltpu.VMEM((2, BLOCK, depth), jnp.int32),
            pltpu.VMEM((groups, width, depth), BF16),
            pltpu.VMEM((2, rows_all, width), BF16),
            pltpu.VMEM((rows_all, width), BF16),
            pltpu.VMEM((rows_all, width), F32),
            pltpu.VMEM((rows_all, width), BF16),
            pltpu.VMEM((groups, rows, width), BF16),
            pltpu.VMEM((2 * n_b, heads, HEAD_DIM, HEAD_DIM), BF16),
            pltpu.VMEM((heads, HEAD_DIM, HEAD_DIM), F32),
            pltpu.VMEM((seq_bits, heads, HEAD_DIM, HEAD_DIM), BF16),
            pltpu.VMEM((seq_bits, heads, HEAD_DIM, HEAD_DIM), BF16),
            pltpu.VMEM((1 + in_bits, QB, QB), F32),
            pltpu.VMEM((rows, depth), F32),
            dma, dma((2,)), dma((2,)),
            dma((7 * chips - 6,)), dma((7 * chips - 6,)),
            dma((groups,)), dma((groups,)),
            dma((seq_bits,)), dma((seq_bits,)),
        ],
        compiler_params=pltpu.CompilerParams(
            collective_id=0, has_side_effects=True, vmem_limit_bytes=67043328
        ),
        name="layer",
    )(tokens, w_proj, w_codes, gain.reshape(1, width), level_weight, scales)


def solution(mesh):
    placed = (
        P("seq", None),
        P(None, None, "mp"),
        P("mp"),
        P(None, "mp", "seq"),
        P("mp", None),
        P("mp", None),
    )
    return jax.shard_map(
        body, mesh=mesh, in_specs=placed, out_specs=P(("seq", "mp"), None), check_vma=False
    )
```

```python
import functools
import math

import jax
import jax.numpy as jnp
from jax import lax
from jax.experimental import pallas as pl
from jax.experimental.pallas import tpu as pltpu
from jax.sharding import PartitionSpec as P

HEAD_DIM = 128
STRETCH = 64
BLOCK = 128
CORES = 2
QB = 256
MESH = pl.DeviceIdType.MESH
F32 = jnp.float32
BF16 = jnp.bfloat16


def dot(a, b):
    return jnp.dot(a, b, preferred_element_type=F32)


def dot_nt(a, b):
    return lax.dot_general(a, b, (((1,), (1,)), ((), ())), preferred_element_type=F32)


def dot_tn(a, b):
    return lax.dot_general(a, b, (((0,), (0,)), ((), ())), preferred_element_type=F32)


def kernel(
    cfg,
    tok_hbm, w_hbm, codes_hbm, gain_ref, lw_ref, scale_ref,
    out_ref,
    tok, wj, wstage, cstage, wfull, kv, q, gate, att, attr, local, tot, snd, rcv, masks, acc,
    tok_sem, w_sem, c_sem, ws_sem, wr_sem, as_sem, ar_sem, ss_sem, sr_sem,
):
    groups, seq_bits, block_bits, in_bits, factors = cfg
    rows_all, width = q.shape
    depth = tok.shape[1]
    heads = width // HEAD_DIM
    rows = rows_all // groups
    chips = groups // CORES
    seq = lax.axis_index("seq")
    mp = lax.axis_index("mp")
    x = mp // CORES
    c = mp % CORES

    def peer(ix, kc):
        return ((x + ix) % chips) * CORES + (c + kc) % CORES

    def source(ix, kc):
        return ((x - ix + chips) % chips) * CORES + (c - kc + CORES) % CORES

    def seq_peer(j):
        bit = (seq // 2**j) % 2
        return seq + 2**j - bit * 2 ** (j + 1)

    crows = cstage.shape[1]
    wrows = wstage.shape[1]
    n_c = width // crows
    n_w = depth // wrows

    def c_copy(i):
        slot = i % 2
        return pltpu.make_async_copy(
            codes_hbm.at[pl.ds(i * crows, crows)], cstage.at[slot], c_sem.at[slot]
        )

    def w_copy(i):
        slot = i % 2
        return pltpu.make_async_copy(
            w_hbm.at[pl.ds(i * wrows, wrows)], wstage.at[slot], w_sem.at[slot]
        )

    for i in range(2):
        c_copy(i).start()
    for i in range(2):
        w_copy(i).start()
    tok_copy = pltpu.make_async_copy(tok_hbm, tok, tok_sem)
    tok_copy.start()

    barrier = pltpu.get_barrier_semaphore()
    for r in range(1, groups):
        pl.semaphore_signal(
            barrier, inc=1, device_id=(seq, peer(r // CORES, r % CORES)), device_id_type=MESH
        )
    for j in range(seq_bits):
        pl.semaphore_signal(barrier, inc=1, device_id=(seq_peer(j), mp), device_id_type=MESH)

    @pl.loop(0, n_c)
    def _(i):
        c_copy(i).wait()
        codes = cstage[i % 2]
        whole = ((codes & 7) | 8) << ((codes >> 3) & 15)
        value = whole.astype(F32)
        value = jnp.where(codes >= 128, -value, value)
        at = pl.ds(pl.multiple_of(i * crows, crows), crows)
        for k in range(depth // BLOCK):
            scale = jnp.left_shift(jnp.int32(1), scale_ref[i, k] + 16).astype(F32) * 2.0**-26
            cols = slice(k * BLOCK, (k + 1) * BLOCK)
            wfull[mp, at, cols] = (value[:, cols] * scale).astype(BF16)

        @pl.when(i + 2 < n_c)
        def _():
            c_copy(i + 2).start()

    hb = QB // 2
    t = lax.broadcasted_iota(jnp.int32, (hb, hb), 1)
    s = lax.broadcasted_iota(jnp.int32, (hb, hb), 0)
    tc = t // STRETCH
    sc = s // STRETCH
    masks[0] = jnp.where((tc == sc) & (s <= t), 1.0, 0.0).astype(F32)
    for j in range(in_bits - 1):
        hit = ((tc // 2**j) % 2 == 1) & (sc // 2**j == tc // 2**j - 1)
        masks[j + 1] = jnp.where(hit, 1.0, 0.0).astype(F32)

    pl.semaphore_wait(barrier, groups - 1 + seq_bits)

    n_x = chips - 1
    parity = seq % 2
    half = width // 2
    piece = half // 2

    def w_send(k, shard, start, size, seq_to, mp_to):
        at = pl.ds(pl.multiple_of(start, piece), size)
        return pltpu.make_async_remote_copy(
            src_ref=wfull.at[shard, at], dst_ref=wfull.at[shard, at],
            send_sem=ws_sem.at[k], recv_sem=wr_sem.at[k],
            device_id=(seq_to, mp_to), device_id_type=MESH,
        )

    def x_part(ix, ch, shard):
        return w_send(2 * (ix - 1) + ch, shard, parity * half + ch * piece, piece, seq, peer(ix, 0))

    def y_part(ix, ch, which):
        k = 2 * n_x + 2 * (ix - 1) + ch
        return w_send(k, source(ix, 0), which * half + ch * piece, piece, seq_peer(0), mp)

    def cx_part(ix, ch, kc):
        k = 4 * n_x + 2 * (ix - 1) + ch
        return w_send(k, source(ix, kc), parity * half + ch * piece, piece, seq, peer(0, 1))

    def cy_part(ix, kc):
        return w_send(6 * n_x + ix - 1, source(ix, kc), (1 - parity) * half, half, seq, peer(0, 1))

    def c_part(shard):
        return w_send(7 * n_x, shard, 0, width, seq, peer(0, 1))

    def relay(ch):
        for ix in range(1, chips):
            x_part(ix, ch, source(ix, 0)).wait_recv()
            y_part(ix, ch, parity).start()
            cx_part(ix, ch, 0).start()

    for ch in range(2):
        for ix in range(1, chips):
            x_part(ix, ch, mp).start()
    c_part(mp).start()

    @pl.loop(0, n_w)
    def _(i):
        w_copy(i).wait()
        wj[:, pl.ds(pl.multiple_of(i * wrows, wrows), wrows), :] = jnp.swapaxes(wstage[i % 2], 0, 1)

        @pl.when(i + 2 < n_w)
        def _():
            w_copy(i + 2).start()

    tok_copy.wait()
    tb = min(512, rows_all)
    n_t = rows_all // tb

    @pl.loop(0, 2 * n_t)
    def _(i):
        part = i // n_t
        at = pl.ds(pl.multiple_of((i % n_t) * tb, tb), tb)
        kv[part, at, :] = dot(tok[at, :], wj[1 + part]).astype(BF16)

    n_b = rows_all // QB

    @pl.loop(0, heads)
    def _(h):
        cols = pl.ds(pl.multiple_of(h * HEAD_DIM, HEAD_DIM), HEAD_DIM)
        level = []
        for b in range(n_b):
            at = pl.ds(b * QB, QB)
            level.append(dot_tn(kv[1, at, cols], kv[0, at, cols]))
        base = 0
        while len(level) > 1:
            for b, state in enumerate(level):
                local[base + b, h] = state.astype(BF16)
            base += len(level)
            level = [level[2 * b] + level[2 * b + 1] for b in range(len(level) // 2)]
        tot[h] = level[0]
        snd[0, h] = level[0].astype(BF16)

    def s_send(j):
        return pltpu.make_async_remote_copy(
            src_ref=snd.at[j], dst_ref=rcv.at[j],
            send_sem=ss_sem.at[j], recv_sem=sr_sem.at[j],
            device_id=(seq_peer(j), mp), device_id_type=MESH,
        )

    s_send(0).start()
    relay(0)

    def exchange(j):
        s_send(j).wait_recv()
        if j + 1 < seq_bits:
            total = tot[...] + rcv[j].astype(F32)
            tot[...] = total
            snd[j + 1] = total.astype(BF16)
            s_send(j + 1).start()

    @pl.loop(0, n_t)
    def _(i):
        at = pl.ds(pl.multiple_of(i * tb, tb), tb)
        q[at, :] = dot(tok[at, :], wj[0]).astype(BF16)
        g = dot(tok[at, :], wj[3])
        gate[at, :] = g / (1.0 + jnp.exp(-g)) * gain_ref[...]
        for j in range(min(seq_bits, n_t)):
            @pl.when(i == j)
            def _(j=j):
                exchange(j)

    for j in range(n_t, seq_bits):
        exchange(j)

    relay(1)

    def a_send(r, target):
        at = pl.ds(pl.multiple_of(target * rows, rows), rows)
        return pltpu.make_async_remote_copy(
            src_ref=att.at[at], dst_ref=attr.at[mp],
            send_sem=as_sem.at[r], recv_sem=ar_sem.at[r],
            device_id=(seq, target), device_id_type=MESH,
        )

    n_in = 1 + in_bits

    @pl.loop(0, groups)
    def _(step):
        r = groups - 1 - step
        owner = peer(r // CORES, r % CORES)

        @pl.loop(0, rows // QB)
        def _(part):
            b = owner * (rows // QB) + part
            at = pl.ds(pl.multiple_of(b * QB, QB), QB)
            for h in range(heads):
                cols = slice(h * HEAD_DIM, (h + 1) * HEAD_DIM)
                qh = q[at, cols]
                vh = kv[1, at, cols]

                def weight(level):
                    return lw_ref[level, h : h + 1, at].astype(F32) * factors[level]

                scores = dot_nt(kv[0, at, cols], qh)

                def corner(lo):
                    side = slice(lo, lo + hb)
                    mix = weight(0)[:, side] * masks[0]
                    for j in range(in_bits - 1):
                        mix = mix + weight(1 + j)[:, side] * masks[1 + j]
                    return (scores[side, side] * mix).astype(BF16)

                upper = (scores[:hb, hb:] * weight(in_bits)[:, hb:]).astype(BF16)
                probs = jnp.concatenate(
                    [
                        jnp.concatenate([corner(0), upper], 1),
                        jnp.concatenate([jnp.zeros((hb, hb), BF16), corner(hb)], 1),
                    ],
                    0,
                )
                qt = qh.astype(F32).T
                left = []
                right = []
                base = 0
                for j in range(block_bits):
                    node = b // 2**j
                    bit = node % 2
                    right.append((qt * (weight(n_in + j) * bit.astype(F32))).astype(BF16))
                    left.append(local[base + node - bit, h])
                    base += n_b >> j
                for j in range(seq_bits):
                    bit = (seq // 2**j) % 2
                    right.append((qt * (weight(n_in + block_bits + j) * bit.astype(F32))).astype(BF16))
                    left.append(rcv[j, h])
                memory = dot_tn(vh, probs) + dot(
                    jnp.concatenate(left, 1), jnp.concatenate(right, 0)
                )
                mean = jnp.mean(memory * memory, axis=0, keepdims=True)
                normed = (memory * lax.rsqrt(mean + 1e-06)).T
                att[at, cols] = (normed * gate[at, cols]).astype(BF16)

        @pl.when(r > 0)
        def _():
            a_send(r, owner).start()

    for ix in range(1, chips):
        for ch in range(2):
            y_part(ix, ch, 1 - parity).wait_recv()
        cy_part(ix, 0).start()

    nb = min(512, depth)

    def product(left, g, first, last):
        @pl.loop(0, depth // nb)
        def _(i):
            cols = pl.ds(pl.multiple_of(i * nb, nb), nb)
            value = dot(left, wfull[g, :, cols])
            if not first:
                value = value + acc[:, cols]
            if last:
                out_ref[:, cols] = value.astype(BF16)
            else:
                acc[:, cols] = value

    own = pl.ds(pl.multiple_of(mp * rows, rows), rows)
    product(att[own, :], mp, True, groups == 1)
    for r in range(1, groups):
        ix, kc = r // CORES, r % CORES
        src = source(ix, kc)
        at = pl.ds(pl.multiple_of(src * rows, rows), rows)
        pltpu.make_async_remote_copy(
            src_ref=att.at[own], dst_ref=attr.at[src],
            send_sem=as_sem.at[r], recv_sem=ar_sem.at[r],
            device_id=(seq, src), device_id_type=MESH,
        ).wait_recv()
        if kc and ix:
            for ch in range(2):
                cx_part(ix, ch, 1).wait_recv()
            cy_part(ix, 1).wait_recv()
        elif kc:
            c_part(src).wait_recv()
        product(attr[src], src, False, r == groups - 1)

    c_part(mp).wait_send()
    for ix in range(1, chips):
        for ch in range(2):
            x_part(ix, ch, mp).wait_send()
            y_part(ix, ch, parity).wait_send()
            cx_part(ix, ch, 0).wait_send()
        cy_part(ix, 0).wait_send()
    for j in range(seq_bits):
        s_send(j).wait_send()
    for r in range(1, groups):
        a_send(r, peer(r // CORES, r % CORES)).wait_send()


def body(tokens, w_proj, gain, level_codes, w_codes, block_exponent):
    rows_all, depth = tokens.shape
    width = w_proj.shape[2]
    heads = width // HEAD_DIM
    groups = lax.axis_size("mp")
    seq_size = lax.axis_size("seq")
    seq_bits = seq_size.bit_length() - 1
    stretch_bits = (rows_all // STRETCH).bit_length() - 1
    in_bits = (QB // STRETCH).bit_length() - 1
    block_bits = stretch_bits - in_bits
    levels = level_codes.shape[0]
    rows = rows_all // groups
    chips = groups // CORES
    spans = [STRETCH] + [STRETCH << j for j in range(levels - 1)]
    factors = [1.0 / 128.0 / math.sqrt(HEAD_DIM * span) for span in spans]
    n_b = rows_all // QB
    vmem = pl.BlockSpec(memory_space=pltpu.VMEM)
    hbm = pl.BlockSpec(memory_space=pl.ANY)
    dma = pltpu.SemaphoreType.DMA
    return pl.pallas_call(
        functools.partial(kernel, (groups, seq_bits, block_bits, in_bits, factors)),
        out_shape=jax.ShapeDtypeStruct((rows, depth), BF16),
        in_specs=[hbm, hbm, hbm, vmem, vmem, pl.BlockSpec(memory_space=pltpu.SMEM)],
        out_specs=vmem,
        scratch_shapes=[
            pltpu.VMEM((rows_all, depth), BF16),
            pltpu.VMEM((4, depth, width), BF16),
            pltpu.VMEM((2, 256, 4, width), BF16),
            pltpu.VMEM((2, BLOCK, depth), jnp.int32),
            pltpu.VMEM((groups, width, depth), BF16),
            pltpu.VMEM((2, rows_all, width), BF16),
            pltpu.VMEM((rows_all, width), BF16),
            pltpu.VMEM((rows_all, width), F32),
            pltpu.VMEM((rows_all, width), BF16),
            pltpu.VMEM((groups, rows, width), BF16),
            pltpu.VMEM((2 * n_b, heads, HEAD_DIM, HEAD_DIM), BF16),
            pltpu.VMEM((heads, HEAD_DIM, HEAD_DIM), F32),
            pltpu.VMEM((seq_bits, heads, HEAD_DIM, HEAD_DIM), BF16),
            pltpu.VMEM((seq_bits, heads, HEAD_DIM, HEAD_DIM), BF16),
            pltpu.VMEM((in_bits, QB // 2, QB // 2), F32),
            pltpu.VMEM((rows, depth), F32),
            dma, dma((2,)), dma((2,)),
            dma((7 * chips - 6,)), dma((7 * chips - 6,)),
            dma((groups,)), dma((groups,)),
            dma((seq_bits,)), dma((seq_bits,)),
        ],
        compiler_params=pltpu.CompilerParams(
            collective_id=0, has_side_effects=True, vmem_limit_bytes=67043328
        ),
        name="layer",
    )(tokens, w_proj, w_codes, gain.reshape(1, width), level_codes, block_exponent)


def solution(mesh):
    placed = (
        P("seq", None),
        P(None, None, "mp"),
        P("mp"),
        P(None, "mp", "seq"),
        P("mp", None),
        P("mp", None),
    )
    return jax.shard_map(
        body, mesh=mesh, in_specs=placed, out_specs=P(("seq", "mp"), None), check_vma=False
    )
```

```python
import functools
import math

import jax
import jax.numpy as jnp
from jax import lax
from jax.experimental import pallas as pl
from jax.experimental.pallas import tpu as pltpu
from jax.sharding import PartitionSpec as P

HEAD_DIM = 128
STRETCH = 64
BLOCK = 128
CORES = 2
QB = 256
MESH = pl.DeviceIdType.MESH
F32 = jnp.float32
BF16 = jnp.bfloat16


def dot(a, b):
    return jnp.dot(a, b, preferred_element_type=F32)


def dot_nt(a, b):
    return lax.dot_general(a, b, (((1,), (1,)), ((), ())), preferred_element_type=F32)


def dot_tn(a, b):
    return lax.dot_general(a, b, (((0,), (0,)), ((), ())), preferred_element_type=F32)


def kernel(
    cfg,
    tok_hbm, w_hbm, codes_hbm, gain_ref, lw_ref, scale_ref,
    out_ref,
    tok, wj, wstage, cstage, wfull, kv, q, gate, att, attr, local, tot, snd, rcv, masks, acc,
    tok_sem, w_sem, c_sem, ws_sem, wr_sem, as_sem, ar_sem, ss_sem, sr_sem,
):
    groups, seq_bits, block_bits, in_bits, factors = cfg
    rows_all, width = q.shape
    depth = tok.shape[1]
    heads = width // HEAD_DIM
    rows = rows_all // groups
    chips = groups // CORES
    seq = lax.axis_index("seq")
    mp = lax.axis_index("mp")
    x = mp // CORES
    c = mp % CORES

    def peer(ix, kc):
        return ((x + ix) % chips) * CORES + (c + kc) % CORES

    def source(ix, kc):
        return ((x - ix + chips) % chips) * CORES + (c - kc + CORES) % CORES

    def seq_peer(j):
        bit = (seq // 2**j) % 2
        return seq + 2**j - bit * 2 ** (j + 1)

    crows = cstage.shape[1]
    wrows = wstage.shape[1]
    n_c = width // crows
    n_w = depth // wrows

    def c_copy(i):
        slot = i % 2
        return pltpu.make_async_copy(
            codes_hbm.at[pl.ds(i * crows, crows)], cstage.at[slot], c_sem.at[slot]
        )

    def w_copy(i):
        slot = i % 2
        return pltpu.make_async_copy(
            w_hbm.at[pl.ds(i * wrows, wrows)], wstage.at[slot], w_sem.at[slot]
        )

    for i in range(2):
        c_copy(i).start()
    for i in range(2):
        w_copy(i).start()
    tok_copy = pltpu.make_async_copy(tok_hbm, tok, tok_sem)
    tok_copy.start()

    barrier = pltpu.get_barrier_semaphore()
    for r in range(1, groups):
        pl.semaphore_signal(
            barrier, inc=1, device_id=(seq, peer(r // CORES, r % CORES)), device_id_type=MESH
        )
    for j in range(seq_bits):
        pl.semaphore_signal(barrier, inc=1, device_id=(seq_peer(j), mp), device_id_type=MESH)

    @pl.loop(0, n_c)
    def _(i):
        c_copy(i).wait()
        codes = cstage[i % 2]
        whole = ((codes & 7) | 8) << ((codes >> 3) & 15)
        value = whole.astype(F32)
        value = jnp.where(codes >= 128, -value, value)
        at = pl.ds(pl.multiple_of(i * crows, crows), crows)
        for k in range(depth // BLOCK):
            scale = jnp.left_shift(jnp.int32(1), scale_ref[i, k] + 16).astype(F32) * 2.0**-26
            cols = slice(k * BLOCK, (k + 1) * BLOCK)
            wfull[mp, at, cols] = (value[:, cols] * scale).astype(BF16)

        @pl.when(i + 2 < n_c)
        def _():
            c_copy(i + 2).start()

    hb = QB // 2
    t = lax.broadcasted_iota(jnp.int32, (hb, hb), 1)
    s = lax.broadcasted_iota(jnp.int32, (hb, hb), 0)
    tc = t // STRETCH
    sc = s // STRETCH
    masks[0] = jnp.where((tc == sc) & (s <= t), 1.0, 0.0).astype(F32)
    for j in range(in_bits - 1):
        hit = ((tc // 2**j) % 2 == 1) & (sc // 2**j == tc // 2**j - 1)
        masks[j + 1] = jnp.where(hit, 1.0, 0.0).astype(F32)

    pl.semaphore_wait(barrier, groups - 1 + seq_bits)

    n_x = chips - 1
    parity = seq % 2
    half = width // 2
    piece = half // 2

    def w_send(k, shard, start, size, seq_to, mp_to):
        at = pl.ds(pl.multiple_of(start, piece), size)
        return pltpu.make_async_remote_copy(
            src_ref=wfull.at[shard, at], dst_ref=wfull.at[shard, at],
            send_sem=ws_sem.at[k], recv_sem=wr_sem.at[k],
            device_id=(seq_to, mp_to), device_id_type=MESH,
        )

    def x_part(ix, ch, shard):
        return w_send(2 * (ix - 1) + ch, shard, parity * half + ch * piece, piece, seq, peer(ix, 0))

    def y_part(ix, ch, which):
        k = 2 * n_x + 2 * (ix - 1) + ch
        return w_send(k, source(ix, 0), which * half + ch * piece, piece, seq_peer(0), mp)

    def cx_part(ix, ch, kc):
        k = 4 * n_x + 2 * (ix - 1) + ch
        return w_send(k, source(ix, kc), parity * half + ch * piece, piece, seq, peer(0, 1))

    def cy_part(ix, kc):
        return w_send(6 * n_x + ix - 1, source(ix, kc), (1 - parity) * half, half, seq, peer(0, 1))

    def c_part(shard):
        return w_send(7 * n_x, shard, 0, width, seq, peer(0, 1))

    def relay(ch):
        for ix in range(1, chips):
            x_part(ix, ch, source(ix, 0)).wait_recv()
            y_part(ix, ch, parity).start()
            cx_part(ix, ch, 0).start()

    for ch in range(2):
        for ix in range(1, chips):
            x_part(ix, ch, mp).start()
    c_part(mp).start()

    @pl.loop(0, n_w)
    def _(i):
        w_copy(i).wait()
        wj[:, pl.ds(pl.multiple_of(i * wrows, wrows), wrows), :] = jnp.swapaxes(wstage[i % 2], 0, 1)

        @pl.when(i + 2 < n_w)
        def _():
            w_copy(i + 2).start()

    tok_copy.wait()
    tb = min(512, rows_all)
    n_t = rows_all // tb

    @pl.loop(0, 2 * n_t)
    def _(i):
        part = i // n_t
        at = pl.ds(pl.multiple_of((i % n_t) * tb, tb), tb)
        kv[part, at, :] = dot(tok[at, :], wj[1 + part]).astype(BF16)

    n_b = rows_all // QB

    @pl.loop(0, heads)
    def _(h):
        cols = pl.ds(pl.multiple_of(h * HEAD_DIM, HEAD_DIM), HEAD_DIM)
        level = []
        for b in range(n_b):
            at = pl.ds(b * QB, QB)
            level.append(dot_tn(kv[1, at, cols], kv[0, at, cols]))
        base = 0
        while len(level) > 1:
            for b, state in enumerate(level):
                local[base + b, h] = state.astype(BF16)
            base += len(level)
            level = [level[2 * b] + level[2 * b + 1] for b in range(len(level) // 2)]
        tot[h] = level[0]
        snd[0, h] = level[0].astype(BF16)

    def s_send(j):
        return pltpu.make_async_remote_copy(
            src_ref=snd.at[j], dst_ref=rcv.at[j],
            send_sem=ss_sem.at[j], recv_sem=sr_sem.at[j],
            device_id=(seq_peer(j), mp), device_id_type=MESH,
        )

    s_send(0).start()

    def exchange(j):
        s_send(j).wait_recv()
        if j + 1 < seq_bits:
            total = tot[...] + rcv[j].astype(F32)
            tot[...] = total
            snd[j + 1] = total.astype(BF16)
            s_send(j + 1).start()

    in_loop = min(seq_bits - 1, n_t)

    @pl.loop(0, n_t)
    def _(i):
        at = pl.ds(pl.multiple_of(i * tb, tb), tb)
        q[at, :] = dot(tok[at, :], wj[0]).astype(BF16)
        g = dot(tok[at, :], wj[3])
        gate[at, :] = g / (1.0 + jnp.exp(-g)) * gain_ref[...]
        for j in range(in_loop):
            @pl.when(i == j)
            def _(j=j):
                exchange(j)
                if j == 0:
                    relay(0)

    if in_loop == 0:
        relay(0)
    relay(1)
    for j in range(in_loop, seq_bits):
        exchange(j)

    n_parts = rows // QB

    def a_send(r, target, part):
        at = pl.ds(pl.multiple_of(target * rows + part * QB, QB), QB)
        to = pl.ds(pl.multiple_of(part * QB, QB), QB)
        return pltpu.make_async_remote_copy(
            src_ref=att.at[at], dst_ref=attr.at[mp, to],
            send_sem=as_sem.at[r * n_parts + part], recv_sem=ar_sem.at[r * n_parts + part],
            device_id=(seq, target), device_id_type=MESH,
        )

    n_in = 1 + in_bits

    @pl.loop(0, groups)
    def _(step):
        r = groups - 1 - step
        owner = peer(r // CORES, r % CORES)

        @pl.loop(0, rows // QB)
        def _(part):
            b = owner * (rows // QB) + part
            at = pl.ds(pl.multiple_of(b * QB, QB), QB)
            for h in range(heads):
                cols = slice(h * HEAD_DIM, (h + 1) * HEAD_DIM)
                qh = q[at, cols]
                vh = kv[1, at, cols]

                def weight(level):
                    return lw_ref[level, h : h + 1, at].astype(F32) * factors[level]

                scores = dot_nt(kv[0, at, cols], qh)

                def corner(lo):
                    side = slice(lo, lo + hb)
                    mix = weight(0)[:, side] * masks[0]
                    for j in range(in_bits - 1):
                        mix = mix + weight(1 + j)[:, side] * masks[1 + j]
                    return (scores[side, side] * mix).astype(BF16)

                upper = (scores[:hb, hb:] * weight(in_bits)[:, hb:]).astype(BF16)
                probs = jnp.concatenate(
                    [
                        jnp.concatenate([corner(0), upper], 1),
                        jnp.concatenate([jnp.zeros((hb, hb), BF16), corner(hb)], 1),
                    ],
                    0,
                )
                qt = qh.astype(F32).T
                left = []
                right = []
                base = 0
                for j in range(block_bits):
                    node = b // 2**j
                    bit = node % 2
                    right.append((qt * (weight(n_in + j) * bit.astype(F32))).astype(BF16))
                    left.append(local[base + node - bit, h])
                    base += n_b >> j
                for j in range(seq_bits):
                    bit = (seq // 2**j) % 2
                    right.append((qt * (weight(n_in + block_bits + j) * bit.astype(F32))).astype(BF16))
                    left.append(rcv[j, h])
                memory = dot_tn(vh, probs) + dot(
                    jnp.concatenate(left, 1), jnp.concatenate(right, 0)
                )
                mean = jnp.mean(memory * memory, axis=0, keepdims=True)
                normed = (memory * lax.rsqrt(mean + 1e-06)).T
                att[at, cols] = (normed * gate[at, cols]).astype(BF16)

            @pl.when(r > 0)
            def _():
                a_send(r, owner, part).start()

    for ix in range(1, chips):
        for ch in range(2):
            y_part(ix, ch, 1 - parity).wait_recv()
        cy_part(ix, 0).start()

    nb = min(512, depth)

    def product(left, g, first, last):
        @pl.loop(0, depth // nb)
        def _(i):
            cols = pl.ds(pl.multiple_of(i * nb, nb), nb)
            value = dot(left, wfull[g, :, cols])
            if not first:
                value = value + acc[:, cols]
            if last:
                out_ref[:, cols] = value.astype(BF16)
            else:
                acc[:, cols] = value

    own = pl.ds(pl.multiple_of(mp * rows, rows), rows)
    product(att[own, :], mp, True, groups == 1)
    for r in range(1, groups):
        ix, kc = r // CORES, r % CORES
        src = source(ix, kc)
        for part in range(n_parts):
            to = pl.ds(part * QB, QB)
            k = r * n_parts + part
            pltpu.make_async_remote_copy(
                src_ref=attr.at[src, to], dst_ref=attr.at[src, to],
                send_sem=as_sem.at[k], recv_sem=ar_sem.at[k],
                device_id=(seq, src), device_id_type=MESH,
            ).wait_recv()
        if kc and ix:
            for ch in range(2):
                cx_part(ix, ch, 1).wait_recv()
            cy_part(ix, 1).wait_recv()
        elif kc:
            c_part(src).wait_recv()
        product(attr[src], src, False, r == groups - 1)

    c_part(mp).wait_send()
    for ix in range(1, chips):
        for ch in range(2):
            x_part(ix, ch, mp).wait_send()
            y_part(ix, ch, parity).wait_send()
            cx_part(ix, ch, 0).wait_send()
        cy_part(ix, 0).wait_send()
    for j in range(seq_bits):
        s_send(j).wait_send()
    for r in range(1, groups):
        for part in range(n_parts):
            a_send(r, peer(r // CORES, r % CORES), part).wait_send()


def body(tokens, w_proj, gain, level_codes, w_codes, block_exponent):
    rows_all, depth = tokens.shape
    width = w_proj.shape[2]
    heads = width // HEAD_DIM
    groups = lax.axis_size("mp")
    seq_size = lax.axis_size("seq")
    seq_bits = seq_size.bit_length() - 1
    stretch_bits = (rows_all // STRETCH).bit_length() - 1
    in_bits = (QB // STRETCH).bit_length() - 1
    block_bits = stretch_bits - in_bits
    levels = level_codes.shape[0]
    rows = rows_all // groups
    chips = groups // CORES
    spans = [STRETCH] + [STRETCH << j for j in range(levels - 1)]
    factors = [1.0 / 128.0 / math.sqrt(HEAD_DIM * span) for span in spans]
    n_b = rows_all // QB
    vmem = pl.BlockSpec(memory_space=pltpu.VMEM)
    hbm = pl.BlockSpec(memory_space=pl.ANY)
    dma = pltpu.SemaphoreType.DMA
    return pl.pallas_call(
        functools.partial(kernel, (groups, seq_bits, block_bits, in_bits, factors)),
        out_shape=jax.ShapeDtypeStruct((rows, depth), BF16),
        in_specs=[hbm, hbm, hbm, vmem, vmem, pl.BlockSpec(memory_space=pltpu.SMEM)],
        out_specs=vmem,
        scratch_shapes=[
            pltpu.VMEM((rows_all, depth), BF16),
            pltpu.VMEM((4, depth, width), BF16),
            pltpu.VMEM((2, 256, 4, width), BF16),
            pltpu.VMEM((2, BLOCK, depth), jnp.int32),
            pltpu.VMEM((groups, width, depth), BF16),
            pltpu.VMEM((2, rows_all, width), BF16),
            pltpu.VMEM((rows_all, width), BF16),
            pltpu.VMEM((rows_all, width), F32),
            pltpu.VMEM((rows_all, width), BF16),
            pltpu.VMEM((groups, rows, width), BF16),
            pltpu.VMEM((2 * n_b, heads, HEAD_DIM, HEAD_DIM), BF16),
            pltpu.VMEM((heads, HEAD_DIM, HEAD_DIM), F32),
            pltpu.VMEM((seq_bits, heads, HEAD_DIM, HEAD_DIM), BF16),
            pltpu.VMEM((seq_bits, heads, HEAD_DIM, HEAD_DIM), BF16),
            pltpu.VMEM((in_bits, QB // 2, QB // 2), F32),
            pltpu.VMEM((rows, depth), F32),
            dma, dma((2,)), dma((2,)),
            dma((7 * chips - 6,)), dma((7 * chips - 6,)),
            dma((groups * (rows // QB),)), dma((groups * (rows // QB),)),
            dma((seq_bits,)), dma((seq_bits,)),
        ],
        compiler_params=pltpu.CompilerParams(
            collective_id=0, has_side_effects=True, vmem_limit_bytes=67043328
        ),
        name="layer",
    )(tokens, w_proj, w_codes, gain.reshape(1, width), level_codes, block_exponent)


def solution(mesh):
    placed = (
        P("seq", None),
        P(None, None, "mp"),
        P("mp"),
        P(None, "mp", "seq"),
        P("mp", None),
        P("mp", None),
    )
    return jax.shard_map(
        body, mesh=mesh, in_specs=placed, out_specs=P(("seq", "mp"), None), check_vma=False
    )
```
